32 devices in a mesh: grp: 2 (over y), uly: 4 (over z), blk: 2 (over x), dp: 2 (over core).
Axes of the slice: x: 2, y: 2, z: 4, core: 2. Of those that a mesh axis runs over, the one named last changes fastest.
Arguments:
- query_act: bfloat16 [4, 1024, 2048], P(('grp', 'dp'), ('uly', 'blk')), parts along dimension 0, may hold values from -8 to 8
- key_act: bfloat16 [4, 1024, 2048], P(('grp', 'dp'), ('uly', 'blk')), parts along dimension 0, may hold values from -8 to 8
- value_act: bfloat16 [4, 1024, 2048], P(('grp', 'dp'), ('uly', 'blk')), parts along dimension 0, may hold values from -6 to 6
- out_grad: bfloat16 [4, 1024, 2048], P(('grp', 'dp'), ('uly', 'blk')), parts along dimension 0, may hold values from -6 to 6
- key_blocks: int32 [8, 8], replicated, may hold values from 0 to 7, as said below
Outputs:
- attn_out: bfloat16 [4, 1024, 2048], P(('grp', 'dp'), ('uly', 'blk')), parts along dimension 0
- query_grad: bfloat16 [4, 1024, 2048], P(('grp', 'dp'), ('uly', 'blk')), parts along dimension 0
- key_grad: bfloat16 [4, 1024, 2048], P(('grp', 'dp'), ('uly', 'blk')), parts along dimension 0
- value_grad: bfloat16 [4, 1024, 2048], P(('grp', 'dp'), ('uly', 'blk')), parts along dimension 0
The draws below stay inside these ranges and needn't reach their ends.
There are 2 independent parts, one for each index of `grp`. The reference program is written for one: setup_inputs(seed, part) draws one part's arguments, and reference() takes and returns one part's arrays. A program takes and returns all parts, laid end to end along the dimension named above; an argument that names none is the same for every part. Nothing has to cross between parts.
Inputs may be any that keep to these rules, and one draw needn't show every extreme that they name: `key_blocks`: row i holds 8 different blocks: i - 1, i and i + 1 where they exist, blocks 0 and 7, and random others. Rows 0 and 7 are not read.
All inputs are finite; a program needn't handle non-finite values.
Results may differ from the reference program's by a relative error of at most 0.015.
Values may be sent and summed in bfloat16 or wider, within the bound.
A program may use at most 128 MiB of HBM per device.

```python
import math
from functools import partial
import jax
import jax.numpy as jnp
from jax import lax

H = 16
DH = 128
BLOCK = 128
NSEL = 8
L = 1024
NBLK = 8
SEQS = 2


def paired_fields(base_key):
    key_query, key_keys = jax.random.split(base_key, 2)
    full_shape = (SEQS, L, H * DH)
    raw_query = jnp.clip(jax.random.normal(key_query, full_shape, jnp.float32), -6.0, 6.0)
    raw_keys = jnp.clip(jax.random.normal(key_keys, full_shape, jnp.float32), -6.0, 6.0)
    return (raw_query, raw_keys)


def draw_query_act(key, part):
    return paired_fields(jax.random.fold_in(key, 7))[0].astype(jnp.bfloat16)


def draw_key_act(key, part):
    return paired_fields(jax.random.fold_in(key, 7))[1].astype(jnp.bfloat16)


def draw_key_blocks(key, part):
    block_ids = jnp.arange(NBLK, dtype=jnp.int32)
    noise_vals = jax.random.randint(key, (NBLK, NBLK), 0, 4096, dtype=jnp.int32)
    fixed_set = (jnp.abs(block_ids[None, :] - block_ids[:, None]) <= 1) | (block_ids[None, :] == 0) | (block_ids[None, :] == NBLK - 1)
    rank_score = jnp.where(fixed_set, (1 << 28) + block_ids[None, :], noise_vals * NBLK + block_ids[None, :])
    top_vals, chosen = lax.top_k(rank_score, NSEL)
    return chosen.astype(jnp.int32)


def steps_of(rng, shape, cuts, low, largest):
    loudness = 1.0
    for axis_at, blocks in cuts:
        steps = jax.random.uniform(jax.random.fold_in(jax.random.fold_in(rng, 6), axis_at), (blocks,), jnp.float32, low / len(cuts), largest / len(cuts))
        loudness = loudness * jnp.repeat(jnp.exp(steps), shape[axis_at] // blocks).reshape((-1,) + (1,) * (len(shape) - 1 - axis_at))
    return loudness


def noise(rng, dims, spread, most, cuts=(), kind=jnp.bfloat16):
    loudness = steps_of(rng, dims, cuts, -0.22, 0.18) if cuts else 1.0
    drawn = jax.random.normal(rng, dims, jnp.float32) * spread * loudness
    return jnp.minimum(jnp.maximum(drawn, -most), most).astype(kind)


def setup_inputs(seed: int = 0, part: int = 0) -> dict:
    streams_of = jax.random.split(jax.random.key(seed), 6)
    own_keys = jax.random.split(jax.random.fold_in(streams_of[5], part), 6)
    return {
        "query_act": draw_query_act(jax.random.fold_in(jax.random.fold_in(streams_of[5], part), 71), part),
        "key_act": draw_key_act(jax.random.fold_in(jax.random.fold_in(streams_of[5], part), 71), part),
        "value_act": noise(own_keys[2], (SEQS, L, H * DH), 1.0, 6.0, ((0, 2), (1, 8))),
        "out_grad": noise(own_keys[3], (SEQS, L, H * DH), 1.0, 6.0, ((0, 2), (1, 8))),
        "key_blocks": draw_key_blocks(jax.random.fold_in(streams_of[5], 71), part),
    }


def log_norm(scores):
    row_top = lax.optimization_barrier(jnp.max(scores, axis=-1, keepdims=True))
    return row_top + jnp.log(lax.optimization_barrier(jnp.sum(jnp.exp(scores - row_top), axis=-1, keepdims=True)))

def rounded(array):
    return lax.optimization_barrier(array.astype(jnp.bfloat16)).astype(jnp.float32)

def attend_head(inputs, key_blocks):
    query_rows, key_rows, value_rows, grad_rows = inputs
    inv_root = 1.0 / math.sqrt(DH)
    q_full = query_rows.astype(jnp.float32)
    k_full = key_rows.astype(jnp.float32)
    v_full = value_rows.astype(jnp.float32)
    g_full = grad_rows.astype(jnp.float32)
    q_blk = q_full.reshape(NBLK, BLOCK, DH)
    g_blk = g_full.reshape(NBLK, BLOCK, DH)
    k_sel = k_full.reshape(NBLK, BLOCK, DH)[key_blocks].reshape(NBLK, NSEL * BLOCK, DH)
    v_sel = v_full.reshape(NBLK, BLOCK, DH)[key_blocks].reshape(NBLK, NSEL * BLOCK, DH)
    scores = jnp.einsum('nbd,nkd->nbk', q_blk, k_sel) * inv_root
    prob_full = jnp.exp(scores - log_norm(scores))
    prob_half = rounded(prob_full)
    out_sparse = jnp.einsum('nbk,nkd->nbd', prob_half, v_sel)
    ends = jnp.array([0, NBLK - 1], dtype=jnp.int32)
    glob_q = q_blk[ends]
    glob_g = g_blk[ends]
    glob_scores = jnp.einsum('gbd,kd->gbk', glob_q, k_full) * inv_root
    glob_prob = jnp.exp(glob_scores - log_norm(glob_scores))
    glob_half = rounded(glob_prob)
    glob_out = jnp.einsum('gbk,kd->gbd', glob_half, v_full)
    out_all = out_sparse.at[0].set(glob_out[0]).at[NBLK - 1].set(glob_out[1])
    out_half = out_all.astype(jnp.bfloat16)
    out_back = lax.optimization_barrier(out_half).astype(jnp.float32)
    row_delta = lax.optimization_barrier(jnp.sum(g_blk * out_back, axis=-1))
    keep_rows = jnp.ones((NBLK,), jnp.float32).at[0].set(0.0).at[NBLK - 1].set(0.0)[:, None, None]
    grad_prob = jnp.einsum('nbd,nkd->nbk', g_blk, v_sel)
    grad_score = rounded(prob_full * (grad_prob - row_delta[..., None]) * keep_rows)
    dq_sparse = jnp.einsum('nbk,nkd->nbd', grad_score, k_sel) * inv_root
    dk_sel = jnp.einsum('nbk,nbd->nkd', grad_score, q_blk) * inv_root
    dv_sel = jnp.einsum('nbk,nbd->nkd', prob_half * keep_rows, g_blk)
    key_acc = jnp.zeros((NBLK, BLOCK, DH), jnp.float32).at[key_blocks].add(dk_sel.reshape(NBLK, NSEL, BLOCK, DH))
    value_acc = jnp.zeros((NBLK, BLOCK, DH), jnp.float32).at[key_blocks].add(dv_sel.reshape(NBLK, NSEL, BLOCK, DH))
    glob_delta = row_delta[ends]
    glob_gprob = jnp.einsum('gbd,kd->gbk', glob_g, v_full)
    glob_score = rounded(glob_prob * (glob_gprob - glob_delta[..., None]))
    glob_dq = jnp.einsum('gbk,kd->gbd', glob_score, k_full) * inv_root
    key_acc = key_acc + (jnp.einsum('gbk,gbd->kd', glob_score, glob_q) * inv_root).reshape(NBLK, BLOCK, DH)
    value_acc = value_acc + jnp.einsum('gbk,gbd->kd', glob_half, glob_g).reshape(NBLK, BLOCK, DH)
    dq_all = dq_sparse.at[0].set(glob_dq[0]).at[NBLK - 1].set(glob_dq[1])
    return (out_half.reshape(L, DH), dq_all.astype(jnp.bfloat16).reshape(L, DH), key_acc.astype(jnp.bfloat16).reshape(L, DH), value_acc.astype(jnp.bfloat16).reshape(L, DH))

def split_heads(array):
    return array.reshape(SEQS, L, H, DH).transpose(0, 2, 1, 3).reshape(SEQS * H, L, DH)

def join_heads(array):
    return array.reshape(SEQS, H, L, DH).transpose(0, 2, 1, 3).reshape(SEQS, L, H * DH)

def reference(query_act, key_act, value_act, out_grad, key_blocks):
    results = lax.map(partial(attend_head, key_blocks=key_blocks), (split_heads(query_act), split_heads(key_act), split_heads(value_act), split_heads(out_grad)))
    return (join_heads(results[0]), join_heads(results[1]), join_heads(results[2]), join_heads(results[3]))
```

```python
import functools
import math

import jax
import jax.numpy as jnp
from jax import lax
from jax.experimental import pallas as pl
from jax.experimental.pallas import tpu as pltpu
from jax.sharding import PartitionSpec as P

DH = 128
BLOCK = 128


def log_norm(scores):
    row_top = jnp.max(scores, axis=-1, keepdims=True)
    return row_top + jnp.log(jnp.sum(jnp.exp(scores - row_top), axis=-1, keepdims=True))


def dense_rows(row_q, row_g, key_all, value_all, inv_root):
    scores = (
        jnp.einsum("rhbd,hkd->rhbk", row_q, key_all, preferred_element_type=jnp.float32) * inv_root
    )
    prob_full = jnp.exp(scores - log_norm(scores))
    prob_half = prob_full.astype(jnp.bfloat16)
    row_out = jnp.einsum(
        "rhbk,hkd->rhbd", prob_half, value_all, preferred_element_type=jnp.float32
    ).astype(jnp.bfloat16)
    row_delta = jnp.sum(row_g.astype(jnp.float32) * row_out.astype(jnp.float32), axis=-1)[..., None]
    grad_prob = jnp.einsum("rhbd,hkd->rhbk", row_g, value_all, preferred_element_type=jnp.float32)
    grad_score = (prob_full * (grad_prob - row_delta)).astype(jnp.bfloat16)
    row_dq = (
        jnp.einsum("rhbk,hkd->rhbd", grad_score, key_all, preferred_element_type=jnp.float32)
        * inv_root
    ).astype(jnp.bfloat16)
    key_part = (
        jnp.einsum("rhbk,rhbd->hkd", grad_score, row_q, preferred_element_type=jnp.float32)
        * inv_root
    )
    value_part = jnp.einsum("rhbk,rhbd->hkd", prob_half, row_g, preferred_element_type=jnp.float32)
    return (row_out, row_dq, key_part, value_part)


def local(query_act, key_act, value_act, out_grad, key_blocks):
    inv_root = 1.0 / math.sqrt(DH)
    uly_count = lax.axis_size("uly")
    blk_count = lax.axis_size("blk")
    cycle_pos = lax.axis_index("blk")
    tok_dev = query_act.shape[1]
    feat_width = query_act.shape[2]
    head_loc = feat_width // uly_count // DH
    sel_count = key_blocks.shape[1]
    q_heads, k_heads, v_heads, g_heads = (
        lax.all_to_all(query_act, "uly", split_axis=2, concat_axis=1, tiled=True),
        lax.all_to_all(key_act, "uly", split_axis=2, concat_axis=1, tiled=True),
        lax.all_to_all(value_act, "uly", split_axis=2, concat_axis=1, tiled=True),
        lax.all_to_all(out_grad, "uly", split_axis=2, concat_axis=1, tiled=True),
    )
    local_rows = uly_count * tok_dev
    key_count = blk_count * local_rows
    per_span = tok_dev // BLOCK
    local_blocks = local_rows // BLOCK
    all_blocks = key_count // BLOCK
    own_k = k_heads[0].reshape(local_rows, head_loc, DH).transpose(1, 0, 2)
    own_v = v_heads[0].reshape(local_rows, head_loc, DH).transpose(1, 0, 2)
    k_all, v_all = (
        lax.all_gather(own_k, "blk", axis=1, tiled=True),
        lax.all_gather(own_v, "blk", axis=1, tiled=True),
    )
    block_ids = jnp.arange(local_blocks, dtype=jnp.int32)
    global_ids = (block_ids // per_span * blk_count + cycle_pos) * per_span + block_ids % per_span
    listed = jnp.take(key_blocks, global_ids, axis=0)
    span_ids = listed // per_span
    gathered_ids = (
        span_ids % blk_count * local_blocks + span_ids // blk_count * per_span + listed % per_span
    )
    keep_rows = (global_ids != 0) & (global_ids != all_blocks - 1)
    q_blocks = q_heads[0].reshape(local_blocks, BLOCK, head_loc, DH).transpose(0, 2, 1, 3)
    g_blocks = g_heads[0].reshape(local_blocks, BLOCK, head_loc, DH).transpose(0, 2, 1, 3)
    k_blocks = k_all.reshape(head_loc, all_blocks, BLOCK, DH)
    v_blocks = v_all.reshape(head_loc, all_blocks, BLOCK, DH)
    group_size = math.gcd(local_blocks, 16)
    loop_turns = local_blocks // group_size
    block_range = jnp.arange(all_blocks, dtype=jnp.int32)

    def sparse_step(acc_pair, inputs):
        key_acc, value_acc = acc_pair
        q_grp, g_grp, ids_grp, keep_grp = inputs
        picker = ids_grp[:, :, None] == block_range[None, None, :]
        pick_half = picker.astype(jnp.bfloat16)
        pick_full = picker.astype(jnp.float32)
        k_sel = jnp.einsum(
            "gsn,hnbd->ghsbd", pick_half, k_blocks, preferred_element_type=jnp.float32
        ).astype(jnp.bfloat16)
        v_sel = jnp.einsum(
            "gsn,hnbd->ghsbd", pick_half, v_blocks, preferred_element_type=jnp.float32
        ).astype(jnp.bfloat16)
        k_sel = k_sel.reshape(group_size, head_loc, sel_count * BLOCK, DH)
        v_sel = v_sel.reshape(group_size, head_loc, sel_count * BLOCK, DH)
        scores = (
            jnp.einsum("ghbd,ghkd->ghbk", q_grp, k_sel, preferred_element_type=jnp.float32)
            * inv_root
        )
        prob_full = jnp.exp(scores - log_norm(scores))
        prob_half = prob_full.astype(jnp.bfloat16)
        out_grp = jnp.einsum(
            "ghbk,ghkd->ghbd", prob_half, v_sel, preferred_element_type=jnp.float32
        ).astype(jnp.bfloat16)
        row_delta = jnp.sum(g_grp.astype(jnp.float32) * out_grp.astype(jnp.float32), axis=-1)[
            ..., None
        ]
        grad_prob = jnp.einsum("ghbd,ghkd->ghbk", g_grp, v_sel, preferred_element_type=jnp.float32)
        keep_full = keep_grp.astype(jnp.float32)[:, None, None, None]
        grad_score = (prob_full * (grad_prob - row_delta) * keep_full).astype(jnp.bfloat16)
        dq_grp = (
            jnp.einsum("ghbk,ghkd->ghbd", grad_score, k_sel, preferred_element_type=jnp.float32)
            * inv_root
        ).astype(jnp.bfloat16)
        dk_sel = (
            jnp.einsum("ghbk,ghbd->ghkd", grad_score, q_grp, preferred_element_type=jnp.float32)
            * inv_root
        )
        kept_half = prob_half * keep_grp.astype(jnp.bfloat16)[:, None, None, None]
        dv_sel = jnp.einsum("ghbk,ghbd->ghkd", kept_half, g_grp, preferred_element_type=jnp.float32)
        dk_sel = dk_sel.reshape(group_size, head_loc, sel_count, BLOCK, DH)
        dv_sel = dv_sel.reshape(group_size, head_loc, sel_count, BLOCK, DH)
        key_acc = key_acc + jnp.einsum(
            "gsn,ghsbd->hnbd", pick_full, dk_sel, precision=lax.Precision.HIGHEST
        )
        value_acc = value_acc + jnp.einsum(
            "gsn,ghsbd->hnbd", pick_full, dv_sel, precision=lax.Precision.HIGHEST
        )
        return ((key_acc, value_acc), (out_grp, dq_grp))

    zero_acc = jnp.zeros((head_loc, all_blocks, BLOCK, DH), jnp.float32)
    scan_inputs = (
        q_blocks.reshape(loop_turns, group_size, head_loc, BLOCK, DH),
        g_blocks.reshape(loop_turns, group_size, head_loc, BLOCK, DH),
        gathered_ids.reshape(loop_turns, group_size, sel_count),
        keep_rows.reshape(loop_turns, group_size),
    )
    (key_acc, value_acc), (out_blocks, dq_blocks) = lax.scan(
        sparse_step, (zero_acc, zero_acc), scan_inputs
    )
    out_blocks = out_blocks.reshape(local_blocks, head_loc, BLOCK, DH)
    dq_blocks = dq_blocks.reshape(local_blocks, head_loc, BLOCK, DH)
    holder_rank = (cycle_pos == 0) | (cycle_pos == blk_count - 1)
    slot_index = jnp.where(cycle_pos == 0, 0, local_blocks - 1).astype(jnp.int32)

    def with_rows(carry_state):
        out_b, dq_b, key_b, value_b = carry_state
        row_q = lax.dynamic_slice_in_dim(q_blocks, slot_index, 1, 0)
        row_g = lax.dynamic_slice_in_dim(g_blocks, slot_index, 1, 0)
        row_out, row_dq, key_part, value_part = dense_rows(row_q, row_g, k_all, v_all, inv_root)
        out_b = lax.dynamic_update_slice_in_dim(out_b, row_out, slot_index, 0)
        dq_b = lax.dynamic_update_slice_in_dim(dq_b, row_dq, slot_index, 0)
        key_b = key_b + key_part.reshape(head_loc, all_blocks, BLOCK, DH)
        value_b = value_b + value_part.reshape(head_loc, all_blocks, BLOCK, DH)
        return (out_b, dq_b, key_b, value_b)

    def without_rows(carry_state):
        return carry_state

    out_blocks, dq_blocks, key_acc, value_acc = lax.cond(
        holder_rank, with_rows, without_rows, (out_blocks, dq_blocks, key_acc, value_acc)
    )
    out_heads = out_blocks.transpose(0, 2, 1, 3).reshape(1, local_rows, head_loc * DH)
    dq_heads = dq_blocks.transpose(0, 2, 1, 3).reshape(1, local_rows, head_loc * DH)
    key_rows = key_acc.transpose(1, 2, 0, 3).reshape(key_count, head_loc * DH)
    value_rows = value_acc.transpose(1, 2, 0, 3).reshape(key_count, head_loc * DH)
    key_own, value_own = (
        lax.psum_scatter(
            key_rows.astype(jnp.bfloat16), "blk", scatter_dimension=0, tiled=True
        ).astype(jnp.float32),
        lax.psum_scatter(
            value_rows.astype(jnp.bfloat16), "blk", scatter_dimension=0, tiled=True
        ).astype(jnp.float32),
    )
    key_heads = key_own.astype(jnp.bfloat16).reshape(1, local_rows, head_loc * DH)
    value_heads = value_own.astype(jnp.bfloat16).reshape(1, local_rows, head_loc * DH)
    out_tok, dq_tok, key_tok, value_tok = (
        lax.all_to_all(out_heads, "uly", split_axis=1, concat_axis=2, tiled=True),
        lax.all_to_all(dq_heads, "uly", split_axis=1, concat_axis=2, tiled=True),
        lax.all_to_all(key_heads, "uly", split_axis=1, concat_axis=2, tiled=True),
        lax.all_to_all(value_heads, "uly", split_axis=1, concat_axis=2, tiled=True),
    )
    return (out_tok, dq_tok, key_tok, value_tok)


def peer_of(pos, step, count):
    if count & (count - 1):
        return (pos + step) % count, (pos - step + count) % count
    out, bit = 0, 1
    while bit < count:
        digit = pos // bit % 2
        out = out + bit * (1 - digit if step & bit else digit)
        bit *= 2
    return out, out


def dense_kernel(
    uly_count,
    blk_count,
    head_loc,
    chunk,
    q_ref,
    k_ref,
    v_ref,
    g_ref,
    out_ref,
    dq_ref,
    dk_ref,
    dv_ref,
    held,
    done,
    key_acc,
    value_acc,
    in_send,
    in_recv,
    out_send,
    out_recv,
    own_in,
    own_out,
):
    inv_root = 1.0 / math.sqrt(DH)
    args = (q_ref, k_ref, v_ref, g_ref)
    results = (out_ref, dq_ref, dk_ref, dv_ref)
    tok_dev = q_ref.shape[1]
    rows = held.shape[2]
    z_pos = lax.axis_index("uly")
    x_pos = lax.axis_index("blk")
    me = z_pos * blk_count + x_pos
    peers = []
    for z_step in range(uly_count):
        for x_step in range(blk_count):
            if z_step or x_step:
                z_to, z_from = peer_of(z_pos, z_step, uly_count)
                x_to, x_from = peer_of(x_pos, x_step, blk_count)
                peers.append(
                    (
                        {"uly": z_to, "blk": x_to},
                        z_to * blk_count + x_to,
                        z_from * blk_count + x_from,
                    )
                )

    def tokens(owner):
        return pl.ds(pl.multiple_of(owner * tok_dev, tok_dev), tok_dev)

    def feats(owner, head):
        return pl.ds(pl.multiple_of((owner * head_loc + head) * DH, DH), DH)

    def send_in(i, head, n):
        device, to, _ = peers[n]
        return pltpu.make_async_remote_copy(
            src_ref=args[i].at[0, :, feats(to, head)],
            dst_ref=held.at[i, head, tokens(me), :],
            send_sem=in_send.at[i, head, n],
            recv_sem=in_recv.at[i, head, n],
            device_id=device,
            device_id_type=pl.DeviceIdType.MESH,
        )

    def land_in(i, head, n):
        device, _, source = peers[n]
        return pltpu.make_async_remote_copy(
            src_ref=args[i].at[0, :, feats(me, head)],
            dst_ref=held.at[i, head, tokens(source), :],
            send_sem=in_send.at[i, head, n],
            recv_sem=in_recv.at[i, head, n],
            device_id=device,
            device_id_type=pl.DeviceIdType.MESH,
        )

    def send_out(i, head, n):
        device, to, _ = peers[n]
        return pltpu.make_async_remote_copy(
            src_ref=done.at[i, head, tokens(to), :],
            dst_ref=results[i].at[0, :, feats(me, head)],
            send_sem=out_send.at[i, head, n],
            recv_sem=out_recv.at[i, head, n],
            device_id=device,
            device_id_type=pl.DeviceIdType.MESH,
        )

    def land_out(i, head, n):
        device, _, source = peers[n]
        return pltpu.make_async_remote_copy(
            src_ref=done.at[i, head, tokens(me), :],
            dst_ref=results[i].at[0, :, feats(source, head)],
            send_sem=out_send.at[i, head, n],
            recv_sem=out_recv.at[i, head, n],
            device_id=device,
            device_id_type=pl.DeviceIdType.MESH,
        )

    def keep_in(i, head):
        return pltpu.make_async_copy(
            args[i].at[0, :, feats(me, head)], held.at[i, head, tokens(me), :], own_in.at[i, head]
        )

    def keep_out(i, head):
        return pltpu.make_async_copy(
            done.at[i, head, tokens(me), :],
            results[i].at[0, :, feats(me, head)],
            own_out.at[i, head],
        )

    barrier = pltpu.get_barrier_semaphore()
    for device, _, _ in peers:
        pl.semaphore_signal(
            barrier, inc=1, device_id=device, device_id_type=pl.DeviceIdType.MESH
        )
    pl.semaphore_wait(barrier, len(peers))

    for head in range(head_loc):
        for n in range(len(peers)):
            for i in range(4):
                send_in(i, head, n).start()
        for i in range(4):
            keep_in(i, head).start()

    for head in range(head_loc):
        for i in range(4):
            keep_in(i, head).wait()
        for n in range(len(peers)):
            for i in range(4):
                land_in(i, head, n).wait_recv()
        key_acc[...] = jnp.zeros_like(key_acc)
        value_acc[...] = jnp.zeros_like(value_acc)

        def step(c, carry, head=head):
            here = pl.ds(pl.multiple_of(c * chunk, chunk), chunk)
            q = held[0, head, here, :]
            k = held[1, head]
            v = held[2, head]
            g = held[3, head, here, :]
            over_feats = (((1,), (1,)), ((), ()))
            over_rows = (((0,), (0,)), ((), ()))
            scores = lax.dot_general(q, k, over_feats, preferred_element_type=jnp.float32)
            scores = scores * inv_root
            powers = jnp.exp(scores - jnp.max(scores, axis=-1, keepdims=True))
            prob_full = powers * (1.0 / jnp.sum(powers, axis=-1, keepdims=True))
            prob_half = prob_full.astype(jnp.bfloat16)
            out = jnp.dot(prob_half, v, preferred_element_type=jnp.float32).astype(jnp.bfloat16)
            row_delta = jnp.sum(
                g.astype(jnp.float32) * out.astype(jnp.float32), axis=-1, keepdims=True
            )
            grad_prob = lax.dot_general(g, v, over_feats, preferred_element_type=jnp.float32)
            grad_score = (prob_full * (grad_prob - row_delta)).astype(jnp.bfloat16)
            dq = jnp.dot(grad_score, k, preferred_element_type=jnp.float32) * inv_root
            done[0, head, here, :] = out
            done[1, head, here, :] = dq.astype(jnp.bfloat16)
            key_acc[...] += lax.dot_general(
                grad_score, q, over_rows, preferred_element_type=jnp.float32
            )
            value_acc[...] += lax.dot_general(
                prob_half, g, over_rows, preferred_element_type=jnp.float32
            )
            return carry

        lax.fori_loop(0, rows // chunk, step, 0)
        done[2, head] = (key_acc[...] * inv_root).astype(jnp.bfloat16)
        done[3, head] = value_acc[...].astype(jnp.bfloat16)
        for n in range(len(peers)):
            for i in range(4):
                send_out(i, head, n).start()
        for i in range(4):
            keep_out(i, head).start()

    for head in range(head_loc):
        for i in range(4):
            keep_out(i, head).wait()
        for n in range(len(peers)):
            for i in range(4):
                send_in(i, head, n).wait_send()
                send_out(i, head, n).wait_send()
                land_out(i, head, n).wait_recv()


def layer(query_act, key_act, value_act, out_grad, key_blocks):
    uly_count = lax.axis_size("uly")
    blk_count = lax.axis_size("blk")
    ranks = uly_count * blk_count
    _, tok_dev, feat_width = query_act.shape
    rows = ranks * tok_dev
    if (feat_width // DH) % ranks or key_blocks.shape[1] * BLOCK != rows:
        return local(query_act, key_act, value_act, out_grad, key_blocks)
    head_loc = feat_width // DH // ranks
    chunk = math.gcd(rows, 256)
    whole = pl.BlockSpec(memory_space=pl.ANY)
    pairs = (4, head_loc, ranks - 1)
    return tuple(
        pl.pallas_call(
            functools.partial(dense_kernel, uly_count, blk_count, head_loc, chunk),
            out_shape=[jax.ShapeDtypeStruct(query_act.shape, jnp.bfloat16)] * 4,
            in_specs=[whole] * 4,
            out_specs=[whole] * 4,
            scratch_shapes=[
                pltpu.VMEM((4, head_loc, rows, DH), jnp.bfloat16),
                pltpu.VMEM((4, head_loc, rows, DH), jnp.bfloat16),
                pltpu.VMEM((rows, DH), jnp.float32),
                pltpu.VMEM((rows, DH), jnp.float32),
                pltpu.SemaphoreType.DMA(pairs),
                pltpu.SemaphoreType.DMA(pairs),
                pltpu.SemaphoreType.DMA(pairs),
                pltpu.SemaphoreType.DMA(pairs),
                pltpu.SemaphoreType.DMA((4, head_loc)),
                pltpu.SemaphoreType.DMA((4, head_loc)),
            ],
            compiler_params=pltpu.CompilerParams(
                collective_id=0, has_side_effects=True, vmem_limit_bytes=60 * 1024 * 1024
            ),
        )(query_act, key_act, value_act, out_grad)
    )


def solution(mesh):
    return jax.shard_map(
        layer,
        mesh=mesh,
        in_specs=(
            P(("grp", "dp"), ("uly", "blk"), None),
            P(("grp", "dp"), ("uly", "blk"), None),
            P(("grp", "dp"), ("uly", "blk"), None),
            P(("grp", "dp"), ("uly", "blk"), None),
            P(),
        ),
        out_specs=(
            P(("grp", "dp"), ("uly", "blk"), None),
            P(("grp", "dp"), ("uly", "blk"), None),
            P(("grp", "dp"), ("uly", "blk"), None),
            P(("grp", "dp"), ("uly", "blk"), None),
        ),
        check_vma=False,
    )
```
